1024 devices in a mesh: dp: 8 (over z_hi, x), blk: 16 (over z_lo, core), resp: 8 (over y).
Axes of the slice: x: 4, y: 8, z: 16 (z_hi: 2, z_lo: 8; z = z_hi * 8 + z_lo), core: 2. Of those that a mesh axis runs over, the one named last changes fastest.
Arguments:
- saved: bfloat16 [8, 2048, 3, 1280], P('dp', 'blk', None, 'resp'), may hold values from -24 to 24
- prefix_cot: bfloat16 [8, 8, 2048, 1280], P('dp', 'resp', 'blk'), may hold values from -24 to 24
- w_out: bfloat16 [1280, 1280], P('resp'), may hold values from -0.15625 to 0.15625
- lengths: int32 [8, 16], P('dp', 'resp'), may hold values from 1 to 512, 4096 in all within a row
- adv_mask: int32 [8, 16, 512], P('dp', 'resp'), may hold values from -3 to 3, as said below
- patch_map: int32 [8, 16, 128], P('dp', 'blk'), may hold values from 0 to 127, each once within a row
Outputs:
- grad_qkv: bfloat16 [8, 2048, 3, 1280], P('dp', 'blk', None, 'resp')
The draws below stay inside these ranges and needn't reach their ends.
Inputs may be any that keep to these rules, and one draw needn't show every extreme that they name: `adv_mask`: within one response every nonzero entry has the same value. The 16 lengths of one image sum to 4096; the longest is 512. `patch_map`: each row of 128 entries holds every number of 0 to 127 once.
All inputs are finite; a program needn't handle non-finite values. No bound on the sum of `lengths` on one device may be relied on, other than what follows from the above.
Results may differ from the reference program's by a relative error of at most 0.03.
Values may be sent and summed in bfloat16 or wider, within the bound.
No kernel may reach another device: no remote copies, remote signals or barrier semaphores. Data moves between devices by JAX's collectives and lax.ppermute only.
A program may use at most 32 MiB of HBM per device.

```python
import math
import jax
import jax.numpy as jnp
import numpy as np
from jax import lax

VD = 1280
HEADS = 16
HD = 80
PB = 128
MAXLEN = 512
RESP_DEV = 2
IMAGES = 8
BLOCKS = 16
GROUPS = 8
PATCHES = 2048
RESPONSES = 16
LEN_TOTAL = 4096


def draw_saved(key, part):
    base_key = jax.random.fold_in(key, 0)
    data = jnp.clip(jax.random.normal(base_key, (IMAGES, PATCHES, 3, VD), jnp.float32), -4.0, 4.0) * 1.3
    return data.astype(jnp.bfloat16)


def draw_adv_mask(key, part):
    level_key, sign_key, mask_key = jax.random.split(key, 3)
    level = jax.random.randint(level_key, (IMAGES, RESPONSES, 1), 1, 4)
    sign = jax.random.randint(sign_key, (IMAGES, RESPONSES, 1), 0, 2) * 2 - 1
    marks = jax.random.randint(mask_key, (IMAGES, RESPONSES, MAXLEN), 0, 2)
    return (level * sign * marks).astype(jnp.int32)


def shard_levels(stream_key, dims, cuts, least, high):
    def one(dim, blocks):
        draws = jax.random.uniform(jax.random.fold_in(jax.random.fold_in(stream_key, 6), dim), (blocks,), jnp.float32, least / len(cuts), high / len(cuts))
        return jnp.repeat(jnp.exp(draws), dims[dim] // blocks).reshape((-1,) + (1,) * (len(dims) - dim - 1))

    gain = one(*cuts[0])
    for cut in cuts[1:]:
        gain = gain * one(*cut)
    return gain


def split_up(number_of, total, bound, lean):
    portions = [(1 << 20) // math.isqrt(standing ** lean) + 1 for standing in range(2, number_of + 1)]
    rest, holding = total - bound - (number_of - 1), [1] * (number_of - 1)
    while rest > 0:
        candidates = [i for i in range(number_of - 1) if holding[i] < bound]
        pool, budget = sum([portions[i] for i in candidates]), rest
        for i in candidates:
            extra = min(bound - holding[i], max(1, budget * portions[i] // pool), rest)
            holding[i] = holding[i] + extra
            rest = rest - extra
    return np.array([bound] + holding)


def ragged(key, number_of, total, bound, skew):
    if number_of == 2:
        one = jax.random.randint(key, (), max(1, total - bound), min(bound, total - 1) + 1)
        return jnp.stack([one, total - one])
    sizes = jnp.asarray(split_up(number_of, total, bound, skew), jnp.int32)
    pairs = (number_of - 1) // 2
    giver, receiver = sizes[1:1 + 2 * pairs:2], sizes[2:2 + 2 * pairs:2]
    room = jnp.minimum(giver - 1, bound - receiver)
    shifted = jax.random.randint(jax.random.fold_in(key, 1), (pairs,), 0, 1 << 20) % (room + 1)
    sizes = sizes.at[1:1 + 2 * pairs:2].set(giver - shifted).at[2:2 + 2 * pairs:2].set(receiver + shifted)
    return sizes[jax.random.permutation(jax.random.fold_in(key, 2), number_of)]


def bell_draw(own_key, shape, width, limit, cuts=(), kind=jnp.bfloat16):
    level = shard_levels(own_key, shape, cuts, -0.22, 0.18) if cuts else 1.0
    entries = jax.random.normal(own_key, shape, jnp.float32) * width * level
    return jnp.minimum(jnp.maximum(entries, -limit), limit).astype(kind)


def setup_inputs(seed: int = 0) -> dict:
    key_of = jax.random.split(jax.random.key(seed), 7)
    saved = draw_saved(jax.random.fold_in(key_of[6], 71), 0)
    prefix_cot = bell_draw(key_of[1], (IMAGES, GROUPS, PATCHES, VD), 4.0, 24.0, ((0, 8), (1, 8), (2, 16)))
    w_out = bell_draw(key_of[2], (VD, VD), VD ** -0.5, 0.15625, ((0, 8),))
    lengths = jax.vmap(lambda own: ragged(own, RESPONSES, LEN_TOTAL, MAXLEN, 2))(jax.random.split(key_of[3], IMAGES)).reshape((IMAGES, RESPONSES)).astype(jnp.int32)
    adv_mask = draw_adv_mask(jax.random.fold_in(key_of[6], 71), 0)
    patch_map = jax.vmap(lambda own: jax.random.permutation(own, PB))(jax.random.split(key_of[5], IMAGES * BLOCKS)).reshape((IMAGES, BLOCKS, PB)).astype(jnp.int32)
    return {"saved": saved, "prefix_cot": prefix_cot, "w_out": w_out, "lengths": lengths, "adv_mask": adv_mask, "patch_map": patch_map}


def one_head(item):
    query, keys, values, grad = item
    scale = 1.0 / math.sqrt(HD)
    score = jnp.dot(query, keys.T, preferred_element_type=jnp.float32) * scale
    top = lax.optimization_barrier(jnp.max(score, axis=1))
    expo = jnp.exp(score - top[:, None])
    row_total = lax.optimization_barrier(jnp.sum(expo, axis=1))
    output = (jnp.dot(expo.astype(jnp.bfloat16), values, preferred_element_type=jnp.float32) / row_total[:, None]).astype(jnp.bfloat16)
    log_total = top + jnp.log(row_total)
    delta = lax.optimization_barrier(jnp.sum(grad.astype(jnp.float32) * output.astype(jnp.float32), axis=1))
    prob = jnp.exp(score - log_total[:, None])
    prob_half = prob.astype(jnp.bfloat16)
    dprob = jnp.dot(grad, values.T, preferred_element_type=jnp.float32)
    dscore = (prob * (dprob - delta[:, None])).astype(jnp.bfloat16)
    grad_q = jnp.dot(dscore, keys, preferred_element_type=jnp.float32) * scale
    grad_k = jnp.dot(dscore.T, query, preferred_element_type=jnp.float32) * scale
    grad_v = jnp.dot(prob_half.T, grad, preferred_element_type=jnp.float32)
    return jnp.stack([grad_q, grad_k, grad_v]).astype(jnp.bfloat16)

def to_heads(x):
    return x.reshape(IMAGES, PATCHES, HEADS, HD).transpose(0, 2, 1, 3).reshape(IMAGES * HEADS, PATCHES, HD)

def reference(saved, prefix_cot, w_out, lengths, adv_mask, patch_map):
    live = jnp.arange(MAXLEN, dtype=jnp.int32)[None, None, :] < lengths[:, :, None]
    resp_weight = lax.optimization_barrier(jnp.sum(jnp.where(live, adv_mask, 0).astype(jnp.float32), axis=2)) / MAXLEN
    group_weight = lax.optimization_barrier(jnp.sum(resp_weight.reshape(IMAGES, GROUPS, RESP_DEV), axis=2))
    total = jnp.zeros((IMAGES, PATCHES, VD), jnp.float32)
    for group in range(GROUPS):
        total = total + group_weight[:, group, None, None] * prefix_cot[:, group].astype(jnp.float32)
    total = total.astype(jnp.bfloat16)
    index = (jnp.arange(BLOCKS, dtype=jnp.int32)[None, :, None] * PB + patch_map).reshape(IMAGES, PATCHES).astype(jnp.int32)
    cot_rows = jnp.take_along_axis(total, index[:, :, None], axis=1)
    grad_out = jnp.einsum('ipc,hc->iph', cot_rows.astype(jnp.float32), w_out.astype(jnp.float32)).astype(jnp.bfloat16)
    items = (to_heads(saved[:, :, 0, :]), to_heads(saved[:, :, 1, :]), to_heads(saved[:, :, 2, :]), to_heads(grad_out))
    result = lax.map(one_head, items)
    result = result.reshape(IMAGES, HEADS, 3, PATCHES, HD).transpose(0, 3, 2, 1, 4)
    return result.reshape(IMAGES, PATCHES, 3, VD)
```

```python
import math

import jax
import jax.numpy as jnp
from jax import lax
from jax.experimental import pallas as pl
from jax.experimental.pallas import tpu as pltpu
from jax.sharding import PartitionSpec as P


HD = 80
MAXLEN = 512
LANES = 128
WIDE = 2 * LANES
SCALE = 1.0 / math.sqrt(HD)
SCALE2 = SCALE * math.log2(math.e)
BF = jnp.bfloat16
F32 = jnp.float32

NN = (((1,), (0,)), ((), ()))
NT = (((1,), (1,)), ((), ()))
TN = (((0,), (0,)), ((), ()))


def dot(a, b, dims):
    return lax.dot_general(a, b, dims, preferred_element_type=F32)


def vmem():
    return pl.BlockSpec(memory_space=pltpu.VMEM)


def smem():
    return pl.BlockSpec(memory_space=pltpu.SMEM)


def cost(flops, size):
    return pl.CostEstimate(flops=flops, bytes_accessed=size, transcendentals=0)


def weigh_kernel(len_ref, mask_ref, map_ref, cot_ref, out_ref):
    col = lax.broadcasted_iota(jnp.int32, (1, MAXLEN), 1)
    weight = jnp.zeros((1, 1), F32)
    for r in range(mask_ref.shape[1]):
        live = col < len_ref[0, r]
        marks = jnp.where(live, mask_ref[0, r : r + 1, :], 0).astype(F32)
        weight = weight + jnp.sum(marks, axis=1, keepdims=True) / MAXLEN
    rows = cot_ref.shape[2]
    pick = (lax.broadcasted_iota(jnp.int32, (rows, rows), 0) == map_ref[0]).astype(F32).astype(BF)
    taken = dot(pick, cot_ref[0, 0], TN)
    out_ref[...] = (taken * weight).astype(BF).reshape(out_ref.shape)


def sum_kernel(in_ref, out_ref):
    total = in_ref[0].astype(F32)
    for g in range(1, in_ref.shape[0]):
        total = total + in_ref[g].astype(F32)
    total = total.astype(BF)
    for g in range(out_ref.shape[0]):
        out_ref[g] = total


def grad_kernel(w_ref, rows_ref, out_ref):
    n = rows_ref.shape[0] * rows_ref.shape[1]
    rows = rows_ref[...].reshape(n, rows_ref.shape[2])
    grad = dot(w_ref[...], rows, NT).astype(BF)
    for j in range(out_ref.shape[0]):
        out_ref[j] = grad[(j & 1) * HD : (j & 1) * HD + HD]


def pair(ref, a, b, lo, hi):
    return jnp.concatenate([ref[a, lo:hi, :], ref[b, lo:hi, :]], axis=1)


def forward_kernel(own_ref, oth_ref, kr_ref, vr_ref, kt_ref, out_ref, lse_ref, vt_ref):
    nz = own_ref.shape[0]
    for side, ref in enumerate((own_ref, oth_ref)):
        for s in range(nz):
            span = slice((side * nz + s) * LANES, (side * nz + s + 1) * LANES)
            kr_ref[span, :] = ref[s, HD : 2 * HD, :].T
            vr_ref[span, :] = ref[s, 2 * HD :, :].T
            kt_ref[:, span] = ref[s, HD : 2 * HD, :]
            vt_ref[:, span] = ref[s, 2 * HD :, :]

    def step(j, carry):
        score = dot(kr_ref[...], pair(own_ref, 2 * j, 2 * j + 1, 0, HD), NN)
        top = jnp.max(score, axis=0, keepdims=True)
        expo = jnp.exp2((score - top) * SCALE2)
        total = jnp.sum(expo, axis=0, keepdims=True)
        out = (dot(vt_ref[...], expo.astype(BF), NN) / total).astype(BF)
        lse = top * SCALE2 + jnp.log2(total)
        for e in range(2):
            out_ref[2 * j + e] = out[:, e * LANES : (e + 1) * LANES]
            lse_ref[2 * j + e] = lse[:, e * LANES : (e + 1) * LANES]
        return carry

    lax.fori_loop(0, nz // 2, step, 0)


def backward_kernel(pos_ref, own_ref, kr_ref, vr_ref, kt_ref, o_ref, lse_ref, g_ref, out_ref):
    nz = own_ref.shape[0]
    half = nz * LANES
    chip = pos_ref[0]
    head = pos_ref[1]
    core = pos_ref[2]

    def probs(keys, vals, j):
        a = 2 * j
        query = pair(own_ref, a, a + 1, 0, HD)
        grad = pair(g_ref, chip ^ a, chip ^ (a + 1), 0, HD)
        lse = pair(lse_ref, a, a + 1, 0, 1)
        fwd = pair(o_ref, a, a + 1, 0, HD)
        delta = jnp.sum(grad.astype(F32) * fwd.astype(F32), axis=0, keepdims=True)
        prob = jnp.exp2(dot(keys, query, NN) * SCALE2 - lse)
        dsc = (prob * (dot(vals, grad, NN) - delta)).astype(BF)
        return query, grad, prob.astype(BF), dsc

    _, _, _, dsc = probs(kr_ref[...], vr_ref[...], 0)
    dq = (dot(kt_ref[...], dsc, NN) * SCALE).astype(BF)
    keys = jnp.concatenate([kr_ref[:WIDE, :], kr_ref[half : half + WIDE, :]], axis=0)
    vals = jnp.concatenate([vr_ref[:WIDE, :], vr_ref[half : half + WIDE, :]], axis=0)

    def step(j, acc):
        query, grad, prob, dsc = probs(keys, vals, j)
        return acc[0] + dot(query, dsc, NT), acc[1] + dot(grad, prob, NT)

    zero = jnp.zeros((HD, 2 * WIDE), F32)
    dk, dv = lax.fori_loop(0, nz // 2, step, (zero, zero))
    dk = (dk * SCALE).astype(BF)
    dv = dv.astype(BF)
    for slot in range(2):
        for side in range(2):
            cols = slice(side * WIDE + slot * LANES, side * WIDE + (slot + 1) * LANES)
            dest = 2 * (head ^ slot) + (core ^ side)
            out_ref[dest, :HD, :] = dq[:, slot * LANES : (slot + 1) * LANES]
            out_ref[dest, HD : 2 * HD, :] = dk[:, cols]
            out_ref[dest, 2 * HD :, :] = dv[:, cols]


def make(mesh, interpret=False):
    nresp = mesh.shape["resp"]
    nblk = mesh.shape["blk"]
    nz = nblk // 2
    by_core = [[2 * z + c for z in range(nz)] for c in range(2)]
    quads = [[4 * q + i for i in range(4)] for q in range(nblk // 4)]

    def call(body, outs, n_in, scalars, flops, size, scratch=()):
        in_specs = [smem() if i in scalars else vmem() for i in range(n_in)]
        return pl.pallas_call(
            body,
            out_shape=outs,
            in_specs=in_specs,
            out_specs=jax.tree.map(lambda _: vmem(), outs),
            scratch_shapes=list(scratch),
            cost_estimate=cost(flops, size),
            compiler_params=pltpu.CompilerParams(vmem_limit_bytes=40 * 2**20),
            interpret=interpret,
        )

    def inner(saved, prefix_cot, w_out, lengths, adv_mask, patch_map):
        rows = saved.shape[1]
        model = prefix_cot.shape[3]
        piece = rows // nresp
        sds = jax.ShapeDtypeStruct
        me = lax.axis_index("blk")
        chip, head, core = me >> 1, (me >> 1) & 1, me & 1
        pos = jnp.stack([chip, head, core])

        def hop(x, d):
            return lax.ppermute(x, "blk", [(i, i ^ d) for i in range(nblk)])

        both = saved[0].reshape(rows, 3, 2, HD).transpose(2, 1, 3, 0).reshape(2, 3 * HD, rows)
        mate = hop(lax.dynamic_index_in_dim(both, 1 - head, 0, keepdims=False), 2)

        cot = call(weigh_kernel, sds((nresp, piece, model), BF), 4, (0,), 2 * rows * rows * model, 10**6)(
            lengths, adv_mask, patch_map, prefix_cot
        )
        cot = lax.all_to_all(cot, "resp", 0, 0)
        duo = jnp.stack([lax.dynamic_index_in_dim(both, head, 0, keepdims=False), mate])
        far = [hop(duo, 4 * d) for d in range(1, nz // 2)]
        tot = call(sum_kernel, sds((nresp, piece, model), BF), 1, (), 10**6, 10**6)(cot)
        tot = lax.all_to_all(tot, "resp", 0, 0)
        grad = call(grad_kernel, sds((nz, HD, rows), BF), 2, (), 2 * rows * model * 160, 10**6)(w_out, tot)
        grad = lax.all_to_all(grad, "blk", 0, 0, axis_index_groups=by_core)
        own = jnp.concatenate([duo, *far], axis=0)
        other = hop(own, 1)
        n = nblk * rows
        krows, vrows, kt, fwd, lse = call(
            forward_kernel,
            (
                sds((n, HD), BF),
                sds((n, HD), BF),
                sds((HD, n), BF),
                sds((nz, HD, rows), BF),
                sds((nz, 1, rows), F32),
            ),
            2,
            (),
            4 * n * n * HD,
            4 * 10**6,
            [pltpu.VMEM((HD, n), BF)],
        )(own, other)
        parts = call(backward_kernel, sds((4, 3 * HD, rows), BF), 8, (0,), 5 * n * n * HD, 4 * 10**6)(
            pos, own, krows, vrows, kt, fwd, lse, grad
        )
        parts = lax.all_to_all(parts, "blk", 0, 0, axis_index_groups=quads)

        parts = parts.reshape(2, 2, 3, HD, rows)
        mine = lax.dynamic_index_in_dim(parts[:, :, 0], core, axis=1, keepdims=False)
        sums = (parts[:, 0, 1:].astype(F32) + parts[:, 1, 1:].astype(F32)).astype(BF)
        full = jnp.concatenate([mine[:, None], sums], axis=1)
        return full.transpose(3, 1, 0, 2).reshape(1, rows, 3, 2 * HD)

    in_specs = (
        P("dp", "blk", None, "resp"),
        P("dp", "resp", "blk", None),
        P("resp", None),
        P("dp", "resp"),
        P("dp", "resp", None),
        P("dp", "blk", None),
    )
    out_specs = P("dp", "blk", None, "resp")
    return jax.shard_map(inner, mesh=mesh, in_specs=in_specs, out_specs=out_specs, check_vma=False)


def solution(mesh):
    return make(mesh)
```

```python
import math

import jax
import jax.numpy as jnp
from jax import lax
from jax.experimental import pallas as pl
from jax.experimental.pallas import tpu as pltpu
from jax.sharding import PartitionSpec as P


HD = 80
MAXLEN = 512
LANES = 128
WIDE = 2 * LANES
SCALE = 1.0 / math.sqrt(HD)
SCALE2 = SCALE * math.log2(math.e)
BF = jnp.bfloat16
F32 = jnp.float32

NN = (((1,), (0,)), ((), ()))
NT = (((1,), (1,)), ((), ()))
TN = (((0,), (0,)), ((), ()))


def dot(a, b, dims):
    return lax.dot_general(a, b, dims, preferred_element_type=F32)


def vmem():
    return pl.BlockSpec(memory_space=pltpu.VMEM)


def smem():
    return pl.BlockSpec(memory_space=pltpu.SMEM)


def cost(flops, size):
    return pl.CostEstimate(flops=flops, bytes_accessed=size, transcendentals=0)


def weigh_kernel(len_hbm, mask_hbm, map_hbm, cot_hbm, out_ref, len_ref, mask_ref, map_ref, cot_ref, sems):
    loads = [
        pltpu.make_async_copy(src, dst, sems.at[n])
        for n, (src, dst) in enumerate(
            ((cot_hbm, cot_ref), (mask_hbm, mask_ref), (map_hbm, map_ref), (len_hbm, len_ref))
        )
    ]
    for load in loads:
        load.start()
    for load in loads[1:]:
        load.wait()
    col = lax.broadcasted_iota(jnp.int32, (1, MAXLEN), 1)
    weight = jnp.zeros((1, 1), F32)
    for r in range(mask_ref.shape[1]):
        live = col < len_ref[0:1, r : r + 1]
        marks = jnp.where(live, mask_ref[0, r : r + 1, :], 0).astype(F32)
        weight = weight + jnp.sum(marks, axis=1, keepdims=True) / MAXLEN
    rows = cot_ref.shape[2]
    pick = (lax.broadcasted_iota(jnp.int32, (rows, rows), 0) == map_ref[0]).astype(F32).astype(BF)
    loads[0].wait()
    taken = dot(pick, cot_ref[0, 0], TN)
    out_ref[...] = (taken * weight).astype(BF).reshape(out_ref.shape)


def sum_kernel(in_ref, out_ref):
    total = in_ref[0].astype(F32)
    for g in range(1, in_ref.shape[0]):
        total = total + in_ref[g].astype(F32)
    total = total.astype(BF)
    for g in range(out_ref.shape[0]):
        out_ref[g] = total


def grad_kernel(w_ref, rows_ref, out_ref):
    n = rows_ref.shape[0] * rows_ref.shape[1]
    rows = rows_ref[...].reshape(n, rows_ref.shape[2])
    grad = dot(w_ref[...], rows, NT).astype(BF)
    for j in range(out_ref.shape[0]):
        out_ref[j] = grad[(j & 1) * HD : (j & 1) * HD + HD]


def pair(ref, a, b, lo, hi):
    return jnp.concatenate([ref[a, lo:hi, :], ref[b, lo:hi, :]], axis=1)


def forward_kernel(own_ref, oth_ref, kr_ref, vr_ref, kt_ref, out_ref, lse_ref, vt_ref):
    nz = own_ref.shape[0]
    for side, ref in enumerate((own_ref, oth_ref)):
        for s in range(nz):
            span = slice((side * nz + s) * LANES, (side * nz + s + 1) * LANES)
            kr_ref[span, :] = ref[s, HD : 2 * HD, :].T
            vr_ref[span, :] = ref[s, 2 * HD :, :].T
            kt_ref[:, span] = ref[s, HD : 2 * HD, :]
            vt_ref[:, span] = ref[s, 2 * HD :, :]

    def step(j, carry):
        score = dot(kr_ref[...], pair(own_ref, 2 * j, 2 * j + 1, 0, HD), NN)
        top = jnp.max(score, axis=0, keepdims=True)
        expo = jnp.exp2((score - top) * SCALE2)
        total = jnp.sum(expo, axis=0, keepdims=True)
        out = (dot(vt_ref[...], expo.astype(BF), NN) / total).astype(BF)
        lse = top * SCALE2 + jnp.log2(total)
        for e in range(2):
            out_ref[2 * j + e] = out[:, e * LANES : (e + 1) * LANES]
            lse_ref[2 * j + e] = lse[:, e * LANES : (e + 1) * LANES]
        return carry

    lax.fori_loop(0, nz // 2, step, 0)


def backward_kernel(pos_ref, own_ref, kr_ref, vr_ref, kt_ref, o_ref, lse_ref, g_ref, out_ref):
    nz = own_ref.shape[0]
    half = nz * LANES
    chip = pos_ref[0]
    head = pos_ref[1]
    core = pos_ref[2]

    def probs(keys, vals, j):
        a = 2 * j
        query = pair(own_ref, a, a + 1, 0, HD)
        src = chip ^ (4 * (j & 1) + 2 * (j >> 1))
        grad = pair(g_ref, src, src ^ 1, 0, HD)
        lse = pair(lse_ref, a, a + 1, 0, 1)
        fwd = pair(o_ref, a, a + 1, 0, HD)
        delta = jnp.sum(grad.astype(F32) * fwd.astype(F32), axis=0, keepdims=True)
        prob = jnp.exp2(dot(keys, query, NN) * SCALE2 - lse)
        dsc = (prob * (dot(vals, grad, NN) - delta)).astype(BF)
        return query, grad, prob.astype(BF), dsc

    _, _, _, dsc = probs(kr_ref[...], vr_ref[...], 0)
    dq = (dot(kt_ref[...], dsc, NN) * SCALE).astype(BF)
    keys = jnp.concatenate([kr_ref[:WIDE, :], kr_ref[half : half + WIDE, :]], axis=0)
    vals = jnp.concatenate([vr_ref[:WIDE, :], vr_ref[half : half + WIDE, :]], axis=0)

    def step(j, acc):
        query, grad, prob, dsc = probs(keys, vals, j)
        return acc[0] + dot(query, dsc, NT), acc[1] + dot(grad, prob, NT)

    zero = jnp.zeros((HD, 2 * WIDE), F32)
    dk, dv = lax.fori_loop(0, nz // 2, step, (zero, zero))
    dk = (dk * SCALE).astype(BF)
    dv = dv.astype(BF)
    for slot in range(2):
        for side in range(2):
            cols = slice(side * WIDE + slot * LANES, side * WIDE + (slot + 1) * LANES)
            dest = 2 * (head ^ slot) + (core ^ side)
            out_ref[dest, :HD, :] = dq[:, slot * LANES : (slot + 1) * LANES]
            out_ref[dest, HD : 2 * HD, :] = dk[:, cols]
            out_ref[dest, 2 * HD :, :] = dv[:, cols]


def finish_kernel(pos_ref, in_ref, out_ref):
    core = pos_ref[2]
    for p in range(2):
        span = slice(p * HD, (p + 1) * HD)
        out_ref[0, span, :] = in_ref[2 * p + core, :HD, :]
        for t in range(1, 3):
            rows = slice(t * HD, (t + 1) * HD)
            a, b = in_ref[2 * p, rows, :], in_ref[2 * p + 1, rows, :]
            out_ref[t, span, :] = (a.astype(F32) + b.astype(F32)).astype(BF)


def make(mesh, interpret=False):
    nresp = mesh.shape["resp"]
    nblk = mesh.shape["blk"]
    nz = nblk // 2
    by_core = [[2 * z + c for z in range(nz)] for c in range(2)]
    quads = [[4 * q + i for i in range(4)] for q in range(nblk // 4)]

    def call(body, outs, n_in, scalars, flops, size, scratch=(), raw=False):
        in_specs = [smem() if i in scalars else vmem() for i in range(n_in)]
        if raw:
            in_specs = [pl.BlockSpec(memory_space=pltpu.HBM)] * n_in
        return pl.pallas_call(
            body,
            out_shape=outs,
            in_specs=in_specs,
            out_specs=jax.tree.map(lambda _: vmem(), outs),
            scratch_shapes=list(scratch),
            cost_estimate=cost(flops, size),
            compiler_params=pltpu.CompilerParams(vmem_limit_bytes=(63 if raw else 40) * 2**20),
            interpret=interpret,
        )

    def inner(saved, prefix_cot, w_out, lengths, adv_mask, patch_map):
        rows = saved.shape[1]
        model = prefix_cot.shape[3]
        piece = rows // nresp
        sds = jax.ShapeDtypeStruct
        me = lax.axis_index("blk")
        chip, head, core = me >> 1, (me >> 1) & 1, me & 1
        pos = jnp.stack([chip, head, core])

        def hop(x, d):
            return lax.ppermute(x, "blk", [(i, i ^ d) for i in range(nblk)])

        stage = [
            pltpu.VMEM(lengths.shape, jnp.int32),
            pltpu.VMEM(adv_mask.shape, jnp.int32),
            pltpu.VMEM(patch_map.shape, jnp.int32),
            pltpu.VMEM(prefix_cot.shape, BF),
            pltpu.SemaphoreType.DMA((4,)),
        ]
        cot = call(
            weigh_kernel, sds((nresp, piece, model), BF), 4, (), 2 * rows * rows * model, 10**6, stage, True
        )(lengths, adv_mask, patch_map, prefix_cot)
        cot = lax.all_to_all(cot, "resp", 0, 0)
        both = saved[0].transpose(1, 2, 0)
        lo, hi = both[:, :HD], both[:, HD:]
        kept = jnp.where(head == 0, lo, hi).reshape(3 * HD, rows)
        sent = jnp.where(head == 0, hi, lo).reshape(3 * HD, rows)
        mate = hop(sent, 2)
        duo = jnp.stack([kept, mate])
        quad = hop(duo, 8)
        quad = jnp.concatenate([duo, quad])
        octo = hop(quad, 4)
        tot = call(sum_kernel, sds((nresp, piece, model), BF), 1, (), 10**6, 10**6)(cot)
        tot = lax.all_to_all(tot, "resp", 0, 0)
        grad = call(grad_kernel, sds((nz, HD, rows), BF), 2, (), 2 * rows * model * 160, 10**6)(w_out, tot)
        grad = lax.all_to_all(grad, "blk", 0, 0, axis_index_groups=by_core)
        own = jnp.concatenate([quad, octo])
        other = hop(own, 1)
        n = nblk * rows
        krows, vrows, kt, fwd, lse = call(
            forward_kernel,
            (
                sds((n, HD), BF),
                sds((n, HD), BF),
                sds((HD, n), BF),
                sds((nz, HD, rows), BF),
                sds((nz, 1, rows), F32),
            ),
            2,
            (),
            4 * n * n * HD,
            4 * 10**6,
            [pltpu.VMEM((HD, n), BF)],
        )(own, other)
        parts = call(backward_kernel, sds((4, 3 * HD, rows), BF), 8, (0,), 5 * n * n * HD, 4 * 10**6)(
            pos, own, krows, vrows, kt, fwd, lse, grad
        )
        parts = lax.all_to_all(parts, "blk", 0, 0, axis_index_groups=quads)

        out = call(finish_kernel, sds((3, 2 * HD, rows), BF), 2, (0,), 10**5, 10**6)(pos, parts)
        return out.transpose(2, 0, 1)[None]

    in_specs = (
        P("dp", "blk", None, "resp"),
        P("dp", "resp", "blk", None),
        P("resp", None),
        P("dp", "resp"),
        P("dp", "resp", None),
        P("dp", "blk", None),
    )
    out_specs = P("dp", "blk", None, "resp")
    return jax.shard_map(inner, mesh=mesh, in_specs=in_specs, out_specs=out_specs, check_vma=False)


def solution(mesh):
    return make(mesh)
```
